32 devices in a mesh: batch: 4 (over y, x), tm: 4 (over z), tensor: 2 (over core).
Axes of the slice: x: 2, y: 2, z: 4, core: 2. Of those that a mesh axis runs over, the one named last changes fastest.
Arguments:
- q_raw: bfloat16 [4, 1536, 3072], P('batch', 'tm', 'tensor'), may hold values from -2500 to 2500
- k_raw: bfloat16 [4, 1536, 3072], P('batch', 'tm', 'tensor'), may hold values from -2500 to 2500
- values: bfloat16 [4, 1536, 3072], P('batch', 'tm', 'tensor'), may hold values from -6 to 6
- grad_out: bfloat16 [4, 1536, 3072], P('batch', 'tm', 'tensor'), may hold values from -16 to 16
- gain_q: float32 [3072], P('tensor'), may hold values from 0.25 to 1.75
- gain_k: float32 [3072], P('tensor'), may hold values from 0.25 to 1.75
- tile_lists: int32 [4, 4, 3], P('batch', 'tm'), may hold values from -1 to 3, as said below
Outputs:
- grad_q: bfloat16 [4, 1536, 3072], P('batch', 'tm', 'tensor')
- grad_k: bfloat16 [4, 1536, 3072], P('batch', 'tm', 'tensor')
- grad_values: bfloat16 [4, 1536, 3072], P('batch', 'tm', 'tensor')
- grad_gain_q: float32 [3072], P('tensor')
- grad_gain_k: float32 [3072], P('tensor')
The draws below stay inside these ranges and needn't reach their ends.
Inputs may be any that keep to these rules, and one draw needn't show every extreme that they name: `tile_lists`: every entry is a key tile or -1 for an empty slot. A list names no tile twice, always names its own query tile, and names only tiles whose time slab (tile) differs from the query tile's by at most one; in every clip some list fills all 3 slots.
All inputs are finite; a program needn't handle non-finite values.
Results may differ from the reference program's by a relative error of at most 0.0107.
The reference program's roundings to bfloat16 on the way count: a program that leaves them out, or rounds other values in their place, can miss the bound.
Values may be sent and summed in bfloat16 or wider, within the bound.
A program may use at most 128 MiB of HBM per device.

```python
import math
from functools import partial
import jax
import jax.numpy as jnp
from jax import lax

HEADS = 24
HD = 128
SPT = 1
CLIPS = 4
QT = 4
TOKENS = 1536
WIDTH = 3072
KMAX = 3


def raw_pair(key):
    full_shape = (CLIPS, TOKENS, WIDTH)
    subkeys = jax.random.split(jax.random.fold_in(key, 11), 12)
    head_ids = jnp.arange(WIDTH) // HD
    rising = 1.0 + 2.0 * head_ids.astype(jnp.float32) / max(HEADS - 1, 1)
    head_top = math.log(10.0)
    results = []
    for member in range(2):
        offset = 4 * member
        base_noise = jnp.clip(jax.random.normal(subkeys[offset], full_shape, jnp.float32), -4.0, 4.0)
        row_scale = jnp.exp(jax.random.uniform(subkeys[offset + 1], (CLIPS, TOKENS, 1), jnp.float32, 0.0, math.log(10.0)))
        head_scale = jnp.exp(jax.random.uniform(subkeys[offset + 2], (CLIPS, 1, HEADS), jnp.float32, 0.0, head_top))
        head_cols = jnp.repeat(head_scale, HD, axis=2)
        jitter = jnp.exp(jax.random.uniform(subkeys[offset + 3], (CLIPS, 1, WIDTH), jnp.float32, math.log(0.5), math.log(2.0)))
        results.append(base_noise * row_scale * head_cols * jitter * rising[None, None, :])
    query_part, key_part = (results[0], results[1])
    return (query_part, key_part)


def draw_q_raw(key, part):
    query_part, key_part = raw_pair(key)
    return query_part.astype(jnp.bfloat16)


def draw_k_raw(key, part):
    query_part, key_part = raw_pair(key)
    return key_part.astype(jnp.bfloat16)


def draw_grad_out(key, part):
    subkeys = jax.random.split(jax.random.fold_in(key, 17), 1)
    ordinal = (jnp.arange(CLIPS)[:, None] * TOKENS + jnp.arange(TOKENS)[None, :]).astype(jnp.float32)
    rise_factor = 1.0 + 2.0 * ordinal / (CLIPS * TOKENS - 1)
    base_noise = jnp.clip(jax.random.normal(subkeys[0], (CLIPS, TOKENS, WIDTH), jnp.float32), -4.0, 4.0)
    return (base_noise * rise_factor[:, :, None]).astype(jnp.bfloat16)


def draw_tile_lists(key, part):
    subkeys = jax.random.split(jax.random.fold_in(key, 29), 3)
    spread = min(SPT, 3)
    slab_count = QT // SPT
    query_ids = jnp.arange(QT)
    query_slab = query_ids // SPT
    query_spot = query_ids % SPT
    candidate = jnp.arange(KMAX)
    time_step = candidate // spread - 1
    spot_step = candidate % spread
    window_start = jnp.clip(query_spot - 1, 0, SPT - spread)
    key_slab = query_slab[:, None] + time_step[None, :]
    key_spot = window_start[:, None] + spot_step[None, :]
    tile_ids = key_slab * SPT + key_spot
    exists = (key_slab >= 0) & (key_slab < slab_count)
    itself = (time_step[None, :] == 0) & (key_spot == query_spot[:, None])
    kept_slot = jax.random.randint(subkeys[0], (CLIPS, QT, KMAX), 0, 2) == 1
    full_row = jax.random.randint(subkeys[1], (CLIPS,), SPT, QT - SPT)
    forced = query_ids[None, :, None] == full_row[:, None, None]
    live_entry = exists[None] & (itself[None] | kept_slot | forced)
    entries = jnp.where(live_entry, tile_ids[None], -1)
    ranking = jnp.argsort(jax.random.randint(subkeys[2], (CLIPS, QT, KMAX), 0, 1 << 20) * KMAX + candidate[None, None, :], axis=-1)
    return jnp.take_along_axis(entries, ranking, axis=-1).astype(jnp.int32)


def shard_levels(key, extent, cuts, smallest, high):
    loudness, own = 1.0, jax.random.fold_in(key, 6)
    for dim, blocks in cuts:
        heights = jnp.exp(jax.random.uniform(jax.random.fold_in(own, dim), (blocks,), jnp.float32, smallest / len(cuts), high / len(cuts)))
        loudness = loudness * jnp.repeat(heights, extent[dim] // blocks).reshape([-1 if axis == dim else 1 for axis in range(len(extent))])
    return loudness


def centred(own_key, shape, scale, most, pieces=(), held_as=jnp.bfloat16):
    level = shard_levels(own_key, shape, pieces, -0.22, 0.18) if pieces else 1.0
    drawn = jax.random.normal(own_key, shape, jnp.float32) * scale * level
    return jnp.minimum(jnp.maximum(drawn, -most), most).astype(held_as)


def setup_inputs(seed: int = 0) -> dict:
    arg_keys = jax.random.split(jax.random.key(seed), 8)
    return {
        "q_raw": draw_q_raw(jax.random.fold_in(arg_keys[7], 71), 0),
        "k_raw": draw_k_raw(jax.random.fold_in(arg_keys[7], 71), 0),
        "values": centred(arg_keys[2], (CLIPS, TOKENS, WIDTH), 1.0, 6.0, ((0, 4), (1, 4), (2, 2))),
        "grad_out": draw_grad_out(jax.random.fold_in(arg_keys[7], 71), 0),
        "gain_q": jnp.clip(1.0 + 0.15 * jax.random.normal(arg_keys[4], (WIDTH,), jnp.float32), 0.25, 1.75),
        "gain_k": jnp.clip(1.0 + 0.15 * jax.random.normal(arg_keys[5], (WIDTH,), jnp.float32), 0.25, 1.75),
        "tile_lists": draw_tile_lists(jax.random.fold_in(arg_keys[7], 71), 0),
    }


EPSILON = 1e-06
MASKED_SCORE = -1e+30

def normalize_rows(raw_rows, gain_row):
    wide_rows = raw_rows.astype(jnp.float32)
    inverse = lax.rsqrt(lax.optimization_barrier(jnp.mean(wide_rows * wide_rows, axis=1)) + EPSILON)
    normed = (wide_rows * inverse[:, None] * gain_row[None, :]).astype(jnp.bfloat16)
    return (wide_rows, inverse, normed)

def undo_norm(wide_rows, inverse, gain_row, grad_normed):
    feature_count = wide_rows.shape[1]
    projection = lax.optimization_barrier(jnp.sum(wide_rows * gain_row[None, :] * grad_normed, axis=1))
    cubed = inverse * inverse * inverse
    grad_rows = inverse[:, None] * gain_row[None, :] * grad_normed - wide_rows * (cubed * projection / feature_count)[:, None]
    gain_term = lax.optimization_barrier(jnp.sum(grad_normed * wide_rows * inverse[:, None], axis=0))
    return (grad_rows.astype(jnp.bfloat16), gain_term)

def clip_pass(gain_q, gain_k, packed):
    query_raw, key_raw, value_rows, grad_rows, tile_rows = packed
    token_count, feature_count = query_raw.shape
    tile_count, slot_count = tile_rows.shape
    tile_len = token_count // tile_count
    head_count = feature_count // HD
    score_scale = HD ** (-0.5)
    query_wide, inverse_q, query_norm = normalize_rows(query_raw, gain_q)
    key_wide, inverse_k, key_norm = normalize_rows(key_raw, gain_k)
    tile_shape = (tile_count, tile_len, head_count, HD)
    query_tiles = lax.optimization_barrier(query_norm).astype(jnp.float32).reshape(tile_shape)
    key_tiles = lax.optimization_barrier(key_norm).astype(jnp.float32).reshape(tile_shape)
    value_tiles = value_rows.astype(jnp.float32).reshape(tile_shape)
    grad_tiles = grad_rows.astype(jnp.float32).reshape(tile_shape)

    def step(carry, number):
        key_sum, value_sum = carry
        entries = tile_rows[number]
        live_slots = entries >= 0
        safe_slots = jnp.clip(entries, 0, tile_count - 1)
        key_rows = key_tiles[safe_slots].reshape(slot_count * tile_len, head_count, HD)
        val_rows = value_tiles[safe_slots].reshape(slot_count * tile_len, head_count, HD)
        query_rows = query_tiles[number]
        grad_here = grad_tiles[number]
        scores = jnp.einsum('qhd,khd->hqk', query_rows, key_rows) * score_scale
        live_cols = jnp.repeat(live_slots, tile_len)
        scores = jnp.where(live_cols[None, None, :], scores, MASKED_SCORE)
        highest = lax.optimization_barrier(jnp.max(scores, axis=2, keepdims=True))
        exponent = jnp.exp(scores - highest)
        attn_probs = exponent / lax.optimization_barrier(jnp.sum(exponent, axis=2, keepdims=True))
        dprobs = jnp.einsum('qhd,khd->hqk', grad_here, val_rows)
        row_delta = lax.optimization_barrier(jnp.sum(attn_probs * dprobs, axis=2, keepdims=True))
        dscore = lax.optimization_barrier((attn_probs * (dprobs - row_delta)).astype(jnp.bfloat16)).astype(jnp.float32)
        probs_b = lax.optimization_barrier(attn_probs.astype(jnp.bfloat16)).astype(jnp.float32)
        grad_query = jnp.einsum('hqk,khd->qhd', dscore, key_rows) * score_scale
        grad_key = (jnp.einsum('hqk,qhd->khd', dscore, query_rows) * score_scale).reshape(slot_count, tile_len, head_count, HD)
        grad_value = jnp.einsum('hqk,qhd->khd', probs_b, grad_here).reshape(slot_count, tile_len, head_count, HD)
        return ((key_sum.at[safe_slots].add(grad_key), value_sum.at[safe_slots].add(grad_value)), grad_query)
    zero_tiles = jnp.zeros(tile_shape, jnp.float32)
    (key_sum, value_sum), query_grads = lax.scan(step, (zero_tiles, zero_tiles), jnp.arange(tile_count))
    grad_qn = query_grads.reshape(token_count, feature_count)
    grad_kn = key_sum.reshape(token_count, feature_count)
    grad_values = value_sum.reshape(token_count, feature_count).astype(jnp.bfloat16)
    grad_q, terms_q = undo_norm(query_wide, inverse_q, gain_q, grad_qn)
    grad_k, terms_k = undo_norm(key_wide, inverse_k, gain_k, grad_kn)
    return (grad_q, grad_k, grad_values, terms_q, terms_k)

def reference(q_raw, k_raw, values, grad_out, gain_q, gain_k, tile_lists):
    grad_q, grad_k, grad_values, terms_q, terms_k = lax.map(partial(clip_pass, gain_q, gain_k), (q_raw, k_raw, values, grad_out, tile_lists))
    factor_all = 1.0 / math.sqrt(CLIPS * TOKENS)
    return (grad_q, grad_k, grad_values, lax.optimization_barrier(jnp.sum(terms_q, axis=0)) * factor_all, lax.optimization_barrier(jnp.sum(terms_k, axis=0)) * factor_all)
```

```python
import math

import jax
import jax.numpy as jnp
from jax import lax
from jax.experimental import pallas as pl
from jax.experimental.pallas import tpu as pltpu
from jax.sharding import PartitionSpec as P

HD = 128
STATS = 4
EPSILON = 1e-06
DEAD = 1e30
SCALE = HD ** (-0.5)
CHUNKS = 3


def cols_dot(left, right):
    return lax.dot_general(
        left, right, (((1,), (1,)), ((), ())), preferred_element_type=jnp.float32
    )


def rows_dot(left, right):
    return lax.dot_general(
        left, right, (((0,), (0,)), ((), ())), preferred_element_type=jnp.float32
    )


def stats_body(count, *refs):
    key = refs[0][...]
    value = refs[1][...]
    for t in range(count):
        query = refs[2 + t][...]
        grad = refs[2 + count + t][...]
        out = refs[2 + 2 * count + t]
        scores = cols_dot(key, query) * SCALE
        highest = jnp.max(scores, axis=0, keepdims=True)
        exponent = jnp.exp(scores - highest)
        dprobs = cols_dot(value, grad)
        out[0, 0:1, :] = highest
        out[0, 1:2, :] = jnp.sum(exponent, axis=0, keepdims=True)
        out[0, 2:3, :] = jnp.sum(exponent * dprobs, axis=0, keepdims=True)
        out[0, 3:4, :] = jnp.zeros_like(highest)


def partial_stats(key, value, queries, grads):
    rows, width = key.shape
    heads = width // HD
    count = len(queries)
    column = pl.BlockSpec((rows, HD), lambda h: (0, h))
    stat = pl.BlockSpec((1, STATS, rows), lambda h: (h, 0, 0))

    def body(*refs):
        stats_body(count, *refs)

    return pl.pallas_call(
        body,
        grid=(heads,),
        out_shape=[jax.ShapeDtypeStruct((heads, STATS, rows), jnp.float32)] * count,
        in_specs=[column] * (2 + 2 * count),
        out_specs=[stat] * count,
        cost_estimate=pl.CostEstimate(
            flops=4 * count * rows * rows * width,
            bytes_accessed=(2 + 2 * count) * rows * width * 2,
            transcendentals=count * rows * rows * heads,
        ),
        name=f"stats{count}",
    )(key, value, *queries, *grads)


def combine_body(live, own, before, after, to_own, to_before, to_after):
    alive = (live[0] > 0, live[1] > 0)
    highest = own[:, 0:1, :]
    parts = (before, after)
    for flag, part in zip(alive, parts):
        highest = jnp.where(flag, jnp.maximum(highest, part[:, 0:1, :]), highest)
    weight = jnp.exp(own[:, 0:1, :] - highest)
    total = weight * own[:, 1:2, :]
    delta = weight * own[:, 2:3, :]
    for flag, part in zip(alive, parts):
        weight = jnp.exp(jnp.minimum(part[:, 0:1, :] - highest, 0.0))
        total = total + jnp.where(flag, weight * part[:, 1:2, :], 0.0)
        delta = delta + jnp.where(flag, weight * part[:, 2:3, :], 0.0)
    inverse = 1.0 / total
    delta = delta * inverse
    for out in (to_own, to_before, to_after):
        out[:, 1:2, :] = inverse
        out[:, 2:3, :] = delta
        out[:, 3:4, :] = jnp.zeros_like(delta)
    to_own[:, 0:1, :] = highest
    for flag, out in zip(alive, (to_before, to_after)):
        out[:, 0:1, :] = jnp.where(flag, highest, DEAD)


def combine(live, own, before, after):
    whole = pl.BlockSpec(memory_space=pltpu.VMEM)
    return pl.pallas_call(
        combine_body,
        out_shape=[jax.ShapeDtypeStruct(own.shape, own.dtype)] * 3,
        in_specs=[pl.BlockSpec(memory_space=pltpu.SMEM), whole, whole, whole],
        out_specs=[whole] * 3,
        name="combine",
    )(live, own, before, after)


def grads_body(key_ref, value_ref, q0, q1, q2, g0, g1, g2, c0, c1, c2,
               dkey, dvalue, dq0, dq1, dq2):
    key = key_ref[...]
    value = value_ref[...]
    key_total = None
    value_total = None
    for query_ref, grad_ref, stat, out in (
        (q0, g0, c0, dq0), (q1, g1, c1, dq1), (q2, g2, c2, dq2)
    ):
        query = query_ref[...]
        grad = grad_ref[...]
        scores = cols_dot(key, query) * SCALE
        probs = jnp.exp(scores - stat[0, 0:1, :]) * stat[0, 1:2, :]
        dprobs = cols_dot(value, grad)
        dscore = (probs * (dprobs - stat[0, 2:3, :])).astype(jnp.bfloat16)
        probs_b = probs.astype(jnp.bfloat16)
        value_term = jnp.dot(probs_b, grad, preferred_element_type=jnp.float32)
        key_term = jnp.dot(dscore, query, preferred_element_type=jnp.float32)
        value_total = value_term if value_total is None else value_total + value_term
        key_total = key_term if key_total is None else key_total + key_term
        out[...] = (rows_dot(key, dscore).T * SCALE).astype(out.dtype)
    dkey[...] = key_total * SCALE
    dvalue[...] = value_total.astype(dvalue.dtype)


def full_grads(key, value, queries, grads, stats, first, heads):
    rows = key.shape[0]
    column = pl.BlockSpec((rows, HD), lambda h: (0, h + first))
    result = pl.BlockSpec((rows, HD), lambda h: (0, h))
    stat = pl.BlockSpec((1, STATS, rows), lambda h: (h + first, 0, 0))
    width = heads * HD

    def shape(dtype):
        return jax.ShapeDtypeStruct((rows, width), dtype)

    return pl.pallas_call(
        grads_body,
        grid=(heads,),
        out_shape=[
            shape(jnp.float32), shape(jnp.bfloat16), shape(jnp.float32),
            shape(jnp.bfloat16), shape(jnp.bfloat16),
        ],
        in_specs=[column] * 8 + [stat] * 3,
        out_specs=[result] * 5,
        cost_estimate=pl.CostEstimate(
            flops=30 * rows * rows * width,
            bytes_accessed=15 * rows * width * 2,
            transcendentals=3 * rows * rows * heads,
        ),
        name="grads",
    )(key, value, *queries, *grads, *stats)


def finish_norm(wide_rows, inverse, gain_row, grad_normed, projection, feature_count):
    cubed = inverse * inverse * inverse
    grad_rows = (
        inverse[:, None] * gain_row[None, :] * grad_normed
        - wide_rows * (cubed * projection / feature_count)[:, None]
    )
    return grad_rows.astype(jnp.bfloat16)


def shards(q_raw, k_raw, values, grad_out, gain_q, gain_k, tile_lists):
    query_wide = q_raw[0].astype(jnp.float32)
    key_wide = k_raw[0].astype(jnp.float32)
    value_rows = values[0]
    grad_rows = grad_out[0]
    entries = tile_lists[0, 0]
    token_count, feature_count = query_wide.shape
    head_count = feature_count // HD
    width_all = feature_count * lax.axis_size("tensor")
    count_all = lax.axis_size("batch") * lax.axis_size("tm") * token_count
    peers = lax.axis_size("tm")
    up = [(i, i + 1) for i in range(peers - 1)]
    down = [(i + 1, i) for i in range(peers - 1)]

    def shift(to_before, to_after):
        return lax.ppermute(to_after, "tm", up), lax.ppermute(to_before, "tm", down)

    grad_before, grad_after = shift(grad_rows, grad_rows)
    squares = lax.psum(
        (jnp.sum(query_wide * query_wide, axis=1), jnp.sum(key_wide * key_wide, axis=1)), "tensor"
    )
    inverse_q = lax.rsqrt(squares[0] / width_all + EPSILON)
    inverse_k = lax.rsqrt(squares[1] / width_all + EPSILON)
    query_norm = (query_wide * inverse_q[:, None] * gain_q[None, :]).astype(jnp.bfloat16)
    key_norm = (key_wide * inverse_k[:, None] * gain_k[None, :]).astype(jnp.bfloat16)
    query_before, query_after = shift(query_norm, query_norm)
    position = lax.axis_index("tm")
    live = jnp.stack(
        [
            jnp.any((entries >= 0) & (entries == position - 1)),
            jnp.any((entries >= 0) & (entries == position + 1)),
        ]
    ).astype(jnp.int32)

    (own,) = partial_stats(key_norm, value_rows, [query_norm], [grad_rows])
    for_before, for_after = partial_stats(
        key_norm, value_rows, [query_before, query_after], [grad_before, grad_after]
    )
    from_before, from_after = shift(for_before, for_after)
    stat_own, to_before, to_after = combine(live, own, from_before, from_after)
    stat_before, stat_after = shift(to_before, to_after)

    chunks = math.gcd(CHUNKS, head_count)
    heads = head_count // chunks
    key_parts, value_parts, query_parts = [], [], []
    for chunk in range(chunks):
        dkey, dvalue, own_dq, before_dq, after_dq = full_grads(
            key_norm,
            value_rows,
            [query_norm, query_before, query_after],
            [grad_rows, grad_before, grad_after],
            [stat_own, stat_before, stat_after],
            chunk * heads,
            heads,
        )
        back_before, back_after = shift(before_dq, after_dq)
        key_parts.append(dkey)
        value_parts.append(dvalue)
        query_parts.append(
            own_dq + back_before.astype(jnp.float32) + back_after.astype(jnp.float32)
        )
    grad_kn = jnp.concatenate(key_parts, axis=1)
    grad_values = jnp.concatenate(value_parts, axis=1)
    grad_query = jnp.concatenate(query_parts, axis=1)

    local_q = jnp.sum(query_wide * gain_q[None, :] * grad_query, axis=1)
    local_k = jnp.sum(key_wide * gain_k[None, :] * grad_kn, axis=1)
    proj_k = lax.psum(local_k, "tensor")
    proj_q = lax.psum(local_q, "tensor")
    grad_q = finish_norm(query_wide, inverse_q, gain_q, grad_query, proj_q, width_all)
    grad_k = finish_norm(key_wide, inverse_k, gain_k, grad_kn, proj_k, width_all)
    gain_terms = lax.psum(
        (
            jnp.sum(grad_query * query_wide * inverse_q[:, None], axis=0),
            jnp.sum(grad_kn * key_wide * inverse_k[:, None], axis=0),
        ),
        ("batch", "tm"),
    )
    factor_all = 1.0 / math.sqrt(count_all)
    return (
        grad_q[None],
        grad_k[None],
        grad_values[None],
        gain_terms[0] * factor_all,
        gain_terms[1] * factor_all,
    )


def solution(mesh):
    rows = P("batch", "tm", "tensor")
    return jax.shard_map(
        shards,
        mesh=mesh,
        in_specs=(rows, rows, rows, rows, P("tensor"), P("tensor"), P("batch", "tm", None)),
        out_specs=(rows, rows, rows, P("tensor"), P("tensor")),
        check_vma=False,
    )
```

```python
import math

import jax
import jax.numpy as jnp
from jax import lax
from jax.experimental import pallas as pl
from jax.experimental.pallas import tpu as pltpu
from jax.sharding import PartitionSpec as P

HD = 128
STATS = 4
EPSILON = 1e-06
DEAD = 1e30
SCALE = HD ** (-0.5)
GROUP = 2
MESH = pl.DeviceIdType.MESH


def cols_dot(left, right):
    return lax.dot_general(
        left, right, (((1,), (1,)), ((), ())), preferred_element_type=jnp.float32
    )


def rows_dot(left, right):
    return lax.dot_general(
        left, right, (((0,), (0,)), ((), ())), preferred_element_type=jnp.float32
    )


def tile_stats(key, value, query, grad):
    scores = cols_dot(key, query) * SCALE
    highest = jnp.max(scores, axis=0, keepdims=True)
    exponent = jnp.exp(scores - highest)
    dprobs = cols_dot(value, grad)
    total = jnp.sum(exponent, axis=0, keepdims=True)
    weighted = jnp.sum(exponent * dprobs, axis=0, keepdims=True)
    return highest, total, weighted


def attention_body(group, chunks, live, q, k, v, g, dq, dk, dv,
                   rq, rg, st_own, st_out, st_in, co_own, co_out, co_in, dq_out, dq_in,
                   bulk_send, bulk_recv, st_send, st_recv, co_send, co_recv, dq_send, dq_recv):
    rows = q.shape[0]
    span = group * HD
    me = lax.axis_index("tm")
    peers = lax.axis_size("tm")
    has = (me > 0, me < peers - 1)
    target = (jnp.maximum(me - 1, 0), jnp.minimum(me + 1, peers - 1))

    def part(chunk):
        return pl.ds(pl.multiple_of(chunk * span, HD), span)

    def remote(source, sink, send, recv, side):
        return pltpu.make_async_remote_copy(
            src_ref=source, dst_ref=sink, send_sem=send, recv_sem=recv,
            device_id={"tm": target[side]}, device_id_type=MESH,
        )

    def bulk(chunk, side, slot):
        where = part(chunk)
        return (
            remote(g.at[:, where], rg.at[slot, :, where],
                   bulk_send.at[side, 0, chunk], bulk_recv.at[slot, 0, chunk], side),
            remote(q.at[:, where], rq.at[slot, :, where],
                   bulk_send.at[side, 1, chunk], bulk_recv.at[slot, 1, chunk], side),
        )

    def small(out, into, send, recv, chunk, side, slot):
        where = pl.ds(chunk * group, group)
        return remote(out.at[side, where], into.at[slot, where],
                      send.at[side, chunk], recv.at[slot, chunk], side)

    def stat_copy(chunk, side, slot):
        return small(st_out, st_in, st_send, st_recv, chunk, side, slot)

    def comb_copy(chunk, side, slot):
        return small(co_out, co_in, co_send, co_recv, chunk, side, slot)

    def dq_copy(chunk, side, slot):
        where = part(chunk)
        return remote(dq_out.at[side, :, where], dq_in.at[slot, :, where],
                      dq_send.at[side, chunk], dq_recv.at[slot, chunk], side)

    barrier = pltpu.get_barrier_semaphore()
    for side in range(2):
        @pl.when(has[side])
        def _():
            pl.semaphore_signal(barrier, inc=1, device_id={"tm": target[side]}, device_id_type=MESH)
    pl.semaphore_wait(barrier, (me > 0).astype(jnp.int32) + (me < peers - 1).astype(jnp.int32))

    def start_bulk(chunk):
        for side in range(2):
            @pl.when(has[side])
            def _():
                for copy in bulk(chunk, side, 1 - side):
                    copy.start()

    for chunk in range(min(2, chunks)):
        start_bulk(chunk)
    for side in range(2):
        @pl.when(jnp.logical_not(has[side]))
        def _():
            rq[side] = jnp.zeros(rq.shape[1:], rq.dtype)
            rg[side] = jnp.zeros(rg.shape[1:], rg.dtype)
            dq_in[side] = jnp.zeros(dq_in.shape[1:], dq_in.dtype)
            st_in[side] = jnp.zeros(st_in.shape[1:], st_in.dtype)
            co_in[side] = jnp.zeros(co_in.shape[1:], co_in.dtype)

    def column(head):
        return pl.ds(pl.multiple_of(head * HD, HD), HD)

    def put_stats(ref, index, values):
        for row, value in enumerate(values):
            ref[index + (slice(row, row + 1), slice(None))] = value

    def step(s, carry):
        @pl.when(s < chunks)
        def _():
            for side in range(2):
                @pl.when(has[side])
                def _():
                    for copy in bulk(s, side, side):
                        copy.wait_recv()
            for inner in range(group):
                head = s * group + inner
                col = column(head)
                for side in range(2):
                    put_stats(st_out, (side, head), tile_stats(
                        k[:, col], v[:, col], rq[side, :, col], rg[side, :, col]))

        @pl.when((s >= 1) & (s <= chunks))
        def _():
            for side in range(2):
                @pl.when(has[side])
                def _():
                    stat_copy(s - 1, side, side).wait_recv()
            where = pl.ds((s - 1) * group, group)
            alive = (live[0:1, :] > 0.5, live[1:2, :] > 0.5)
            highest = st_own[where, 0:1, :]
            for side in range(2):
                highest = jnp.where(
                    alive[side], jnp.maximum(highest, st_in[side, where, 0:1, :]), highest)
            weight = jnp.exp(st_own[where, 0:1, :] - highest)
            total = weight * st_own[where, 1:2, :]
            delta = weight * st_own[where, 2:3, :]
            for side in range(2):
                weight = jnp.exp(jnp.minimum(st_in[side, where, 0:1, :] - highest, 0.0))
                total = total + jnp.where(alive[side], weight * st_in[side, where, 1:2, :], 0.0)
                delta = delta + jnp.where(alive[side], weight * st_in[side, where, 2:3, :], 0.0)
            inverse = 1.0 / total
            delta = delta * inverse
            co_own[where, 0:1, :] = highest
            co_own[where, 1:2, :] = inverse
            co_own[where, 2:3, :] = delta
            for side in range(2):
                co_out[side, where, 0:1, :] = jnp.where(alive[side], highest, DEAD)
                co_out[side, where, 1:2, :] = inverse
                co_out[side, where, 2:3, :] = delta

        @pl.when(s < chunks)
        def _():
            for side in range(2):
                @pl.when(has[side])
                def _():
                    stat_copy(s, side, 1 - side).start()

            @pl.when(s + 2 < chunks)
            def _():
                start_bulk(s + 2)
            for inner in range(group):
                head = s * group + inner
                col = column(head)
                put_stats(st_own, (head,), tile_stats(k[:, col], v[:, col], q[:, col], g[:, col]))

        @pl.when((s >= 1) & (s <= chunks))
        def _():
            for side in range(2):
                @pl.when(has[side])
                def _():
                    comb_copy(s - 1, side, 1 - side).start()

        @pl.when(s >= 2)
        def _():
            chunk = s - 2
            for side in range(2):
                @pl.when(has[side])
                def _():
                    comb_copy(chunk, side, side).wait_recv()
            for inner in range(group):
                head = chunk * group + inner
                col = column(head)
                key = k[:, col]
                value = v[:, col]
                key_total = None
                value_total = None
                for t in range(3):
                    if t < 2:
                        query, grad, stat = rq[t, :, col], rg[t, :, col], co_in.at[t]
                    else:
                        query, grad, stat = q[:, col], g[:, col], co_own
                    scores = cols_dot(key, query) * SCALE
                    probs = jnp.exp(scores - stat[head, 0:1, :]) * stat[head, 1:2, :]
                    dprobs = cols_dot(value, grad)
                    dscore = (probs * (dprobs - stat[head, 2:3, :])).astype(jnp.bfloat16)
                    probs_b = probs.astype(jnp.bfloat16)
                    value_term = jnp.dot(probs_b, grad, preferred_element_type=jnp.float32)
                    key_term = jnp.dot(dscore, query, preferred_element_type=jnp.float32)
                    value_total = value_term if t == 0 else value_total + value_term
                    key_total = key_term if t == 0 else key_total + key_term
                    result = rows_dot(key, dscore).T * SCALE
                    if t < 2:
                        dq_out[t, :, col] = result.astype(dq_out.dtype)
                    else:
                        dq[:, col] = result
                dk[:, col] = key_total * SCALE
                dv[:, col] = value_total.astype(dv.dtype)
            for side in range(2):
                @pl.when(has[side])
                def _():
                    dq_copy(chunk, side, 1 - side).start()
        return carry

    lax.fori_loop(0, chunks + 2, step, 0)

    def drain(chunk, carry):
        for side in range(2):
            @pl.when(has[side])
            def _():
                dq_copy(chunk, side, side).wait_recv()
        where = part(chunk)
        dq[:, where] = (
            dq[:, where]
            + dq_in[0, :, where].astype(jnp.float32)
            + dq_in[1, :, where].astype(jnp.float32)
        )
        for side in range(2):
            @pl.when(has[side])
            def _():
                for copy in bulk(chunk, side, 1 - side):
                    copy.wait_send()
                stat_copy(chunk, side, 1 - side).wait_send()
                comb_copy(chunk, side, 1 - side).wait_send()
                dq_copy(chunk, side, 1 - side).wait_send()
        return carry

    lax.fori_loop(0, chunks, drain, 0)


def attention(live, query, key, value, grad):
    rows, width = query.shape
    heads = width // HD
    group = math.gcd(GROUP, heads)
    chunks = heads // group
    whole = pl.BlockSpec(memory_space=pltpu.VMEM)
    stat = (heads, STATS, rows)
    dma = pltpu.SemaphoreType.DMA

    def body(*refs):
        attention_body(group, chunks, *refs)

    return pl.pallas_call(
        body,
        out_shape=[
            jax.ShapeDtypeStruct((rows, width), jnp.float32),
            jax.ShapeDtypeStruct((rows, width), jnp.float32),
            jax.ShapeDtypeStruct((rows, width), jnp.bfloat16),
        ],
        in_specs=[whole] * 5,
        out_specs=[whole] * 3,
        scratch_shapes=[
            pltpu.VMEM((2, rows, width), jnp.bfloat16),
            pltpu.VMEM((2, rows, width), jnp.bfloat16),
            pltpu.VMEM(stat, jnp.float32),
            pltpu.VMEM((2,) + stat, jnp.float32),
            pltpu.VMEM((2,) + stat, jnp.float32),
            pltpu.VMEM(stat, jnp.float32),
            pltpu.VMEM((2,) + stat, jnp.float32),
            pltpu.VMEM((2,) + stat, jnp.float32),
            pltpu.VMEM((2, rows, width), jnp.bfloat16),
            pltpu.VMEM((2, rows, width), jnp.bfloat16),
            dma((2, 2, chunks)), dma((2, 2, chunks)),
            dma((2, chunks)), dma((2, chunks)),
            dma((2, chunks)), dma((2, chunks)),
            dma((2, chunks)), dma((2, chunks)),
        ],
        compiler_params=pltpu.CompilerParams(collective_id=0, has_side_effects=True),
        name="attention",
    )(live, query, key, value, grad)


def totals_body(gains, proj, gain_sum, proj_sum, gain_slots, proj_slots,
                gain_send, gain_recv, proj_send, proj_recv):
    tm = lax.axis_size("tm")
    count = lax.axis_size("batch") * tm
    me = lax.axis_index("batch") * tm + lax.axis_index("tm")
    cores = lax.axis_size("tensor")
    core = lax.axis_index("tensor")
    barrier = pltpu.get_barrier_semaphore()

    def gain_peer(i):
        return lax.rem(me + i, count)

    def gain_id(peer):
        return {"batch": lax.div(peer, tm), "tm": lax.rem(peer, tm)}

    def core_peer(i):
        return lax.rem(core + i, cores)

    def greet_gain(i, carry):
        pl.semaphore_signal(barrier, inc=1, device_id=gain_id(gain_peer(i)), device_id_type=MESH)
        return carry

    def greet_core(i, carry):
        pl.semaphore_signal(barrier, inc=1, device_id={"tensor": core_peer(i)}, device_id_type=MESH)
        return carry

    lax.fori_loop(1, count, greet_gain, 0)
    lax.fori_loop(1, cores, greet_core, 0)
    gain_slots[me] = gains[...]
    proj_slots[core] = proj[...]
    pl.semaphore_wait(barrier, count - 1 + cores - 1)

    def gain_copy(slot, peer):
        return pltpu.make_async_remote_copy(
            src_ref=gains, dst_ref=gain_slots.at[slot], send_sem=gain_send.at[peer],
            recv_sem=gain_recv.at[slot], device_id=gain_id(peer), device_id_type=MESH,
        )

    def proj_copy(slot, peer):
        return pltpu.make_async_remote_copy(
            src_ref=proj, dst_ref=proj_slots.at[slot], send_sem=proj_send.at[peer],
            recv_sem=proj_recv.at[slot], device_id={"tensor": peer}, device_id_type=MESH,
        )

    def send_core(i, carry):
        proj_copy(core, core_peer(i)).start()
        return carry

    def send_gain(i, carry):
        gain_copy(me, gain_peer(i)).start()
        return carry

    def end_core(i, carry):
        peer = core_peer(i)
        proj_copy(core, peer).wait_send()
        proj_copy(peer, peer).wait_recv()
        return carry

    def end_gain(i, carry):
        peer = gain_peer(i)
        gain_copy(me, peer).wait_send()
        gain_copy(peer, peer).wait_recv()
        return carry

    lax.fori_loop(1, cores, send_core, 0)
    lax.fori_loop(1, count, send_gain, 0)
    lax.fori_loop(1, cores, end_core, 0)
    lax.fori_loop(1, count, end_gain, 0)
    proj_sum[...] = jnp.sum(proj_slots[...], axis=0)
    gain_sum[...] = jnp.sum(gain_slots[...], axis=0)


def totals(gains, proj):
    count = lax.axis_size("batch") * lax.axis_size("tm")
    cores = lax.axis_size("tensor")
    whole = pl.BlockSpec(memory_space=pltpu.VMEM)
    dma = pltpu.SemaphoreType.DMA
    return pl.pallas_call(
        totals_body,
        out_shape=[
            jax.ShapeDtypeStruct(gains.shape, jnp.float32),
            jax.ShapeDtypeStruct(proj.shape, jnp.float32),
        ],
        in_specs=[whole] * 2,
        out_specs=[whole] * 2,
        scratch_shapes=[
            pltpu.VMEM((count,) + gains.shape, jnp.float32),
            pltpu.VMEM((cores,) + proj.shape, jnp.float32),
            dma((count,)), dma((count,)), dma((cores,)), dma((cores,)),
        ],
        compiler_params=pltpu.CompilerParams(collective_id=1, has_side_effects=True),
        name="totals",
    )(gains, proj)


def finish_norm(wide_rows, inverse, gain_row, grad_normed, projection, feature_count):
    cubed = inverse * inverse * inverse
    grad_rows = (
        inverse[:, None] * gain_row[None, :] * grad_normed
        - wide_rows * (cubed * projection / feature_count)[:, None]
    )
    return grad_rows.astype(jnp.bfloat16)


def shards(q_raw, k_raw, values, grad_out, gain_q, gain_k, tile_lists):
    query_wide = q_raw[0].astype(jnp.float32)
    key_wide = k_raw[0].astype(jnp.float32)
    value_rows = values[0]
    grad_rows = grad_out[0]
    entries = tile_lists[0, 0]
    token_count, feature_count = query_wide.shape
    width_all = feature_count * lax.axis_size("tensor")
    count_all = lax.axis_size("batch") * lax.axis_size("tm") * token_count
    squares = lax.psum(
        (jnp.sum(query_wide * query_wide, axis=1), jnp.sum(key_wide * key_wide, axis=1)), "tensor"
    )
    inverse_q = lax.rsqrt(squares[0] / width_all + EPSILON)
    inverse_k = lax.rsqrt(squares[1] / width_all + EPSILON)
    query_norm = (query_wide * inverse_q[:, None] * gain_q[None, :]).astype(jnp.bfloat16)
    key_norm = (key_wide * inverse_k[:, None] * gain_k[None, :]).astype(jnp.bfloat16)
    position = lax.axis_index("tm")
    live = jnp.stack(
        [
            jnp.any((entries >= 0) & (entries == position - 1)),
            jnp.any((entries >= 0) & (entries == position + 1)),
        ]
    ).astype(jnp.float32)
    live = jnp.broadcast_to(live[:, None], (2, token_count))
    grad_query, grad_kn, grad_values = attention(live, query_norm, key_norm, value_rows, grad_rows)
    gain_terms, proj = totals(
        jnp.stack(
            [
                jnp.sum(grad_query * query_wide * inverse_q[:, None], axis=0),
                jnp.sum(grad_kn * key_wide * inverse_k[:, None], axis=0),
            ]
        ),
        jnp.stack(
            [
                jnp.sum(query_wide * gain_q[None, :] * grad_query, axis=1),
                jnp.sum(key_wide * gain_k[None, :] * grad_kn, axis=1),
            ]
        ),
    )
    grad_q = finish_norm(query_wide, inverse_q, gain_q, grad_query, proj[0], width_all)
    grad_k = finish_norm(key_wide, inverse_k, gain_k, grad_kn, proj[1], width_all)
    factor_all = 1.0 / math.sqrt(count_all)
    return (
        grad_q[None],
        grad_k[None],
        grad_values[None],
        gain_terms[0] * factor_all,
        gain_terms[1] * factor_all,
    )


def solution(mesh):
    rows = P("batch", "tm", "tensor")
    return jax.shard_map(
        shards,
        mesh=mesh,
        in_specs=(rows, rows, rows, rows, P("tensor"), P("tensor"), P("batch", "tm", None)),
        out_specs=(rows, rows, rows, P("tensor"), P("tensor")),
        check_vma=False,
    )
```

```python
import math

import jax
import jax.numpy as jnp
from jax import lax
from jax.experimental import pallas as pl
from jax.experimental.pallas import tpu as pltpu
from jax.sharding import PartitionSpec as P

HD = 128
STATS = 4
EPSILON = 1e-06
DEAD = 1e30
SCALE = HD ** (-0.5)
GROUP = 2
MESH = pl.DeviceIdType.MESH


def cols_dot(left, right):
    return lax.dot_general(
        left, right, (((1,), (1,)), ((), ())), preferred_element_type=jnp.float32
    )


def rows_dot(left, right):
    return lax.dot_general(
        left, right, (((0,), (0,)), ((), ())), preferred_element_type=jnp.float32
    )


def tile_stats(key, value, query, grad):
    scores = cols_dot(key, query) * SCALE
    highest = jnp.max(scores, axis=0, keepdims=True)
    exponent = jnp.exp(scores - highest)
    dprobs = cols_dot(value, grad)
    total = jnp.sum(exponent, axis=0, keepdims=True)
    weighted = jnp.sum(exponent * dprobs, axis=0, keepdims=True)
    return highest, total, weighted


def attention_body(group, chunks, entries, q_raw, k_raw, v, g, gain_q, gain_k, dq, dk, dv, inv,
                   q, k, squares, sq_send, sq_recv, rq, rg, st_own, st_out, st_in, co_own, co_out, co_in, dq_out, dq_in,
                   bulk_send, bulk_recv, st_send, st_recv, co_send, co_recv, dq_send, dq_recv):
    rows, width = q.shape
    span = group * HD
    core = lax.axis_index("tensor")
    cores = lax.axis_size("tensor")
    me = lax.axis_index("tm")
    peers = lax.axis_size("tm")
    has = (me > 0, me < peers - 1)
    target = (jnp.maximum(me - 1, 0), jnp.minimum(me + 1, peers - 1))

    def part(chunk):
        return pl.ds(pl.multiple_of(chunk * span, HD), span)

    def remote(source, sink, send, recv, side):
        return pltpu.make_async_remote_copy(
            src_ref=source, dst_ref=sink, send_sem=send, recv_sem=recv,
            device_id={"tm": target[side]}, device_id_type=MESH,
        )

    def grad_copy(chunk, side, slot):
        where = part(chunk)
        return remote(g.at[:, where], rg.at[slot, :, where],
                      bulk_send.at[side, 0, chunk], bulk_recv.at[slot, 0, chunk], side)

    def query_copy(chunk, side, slot):
        where = part(chunk)
        return remote(q.at[:, where], rq.at[slot, :, where],
                      bulk_send.at[side, 1, chunk], bulk_recv.at[slot, 1, chunk], side)

    def bulk(chunk, side, slot):
        return grad_copy(chunk, side, slot), query_copy(chunk, side, slot)

    def square_copy(slot, peer):
        return pltpu.make_async_remote_copy(
            src_ref=squares.at[slot], dst_ref=squares.at[slot], send_sem=sq_send.at[peer],
            recv_sem=sq_recv.at[slot], device_id={"tensor": peer}, device_id_type=MESH,
        )

    def small(out, into, send, recv, chunk, side, slot):
        where = pl.ds(chunk * group, group)
        return remote(out.at[side, where], into.at[slot, where],
                      send.at[side, chunk], recv.at[slot, chunk], side)

    def stat_copy(chunk, side, slot):
        return small(st_out, st_in, st_send, st_recv, chunk, side, slot)

    def comb_copy(chunk, side, slot):
        return small(co_out, co_in, co_send, co_recv, chunk, side, slot)

    def dq_copy(chunk, side, slot):
        where = part(chunk)
        return remote(dq_out.at[side, :, where], dq_in.at[slot, :, where],
                      dq_send.at[side, chunk], dq_recv.at[slot, chunk], side)

    barrier = pltpu.get_barrier_semaphore()
    for side in range(2):
        @pl.when(has[side])
        def _():
            pl.semaphore_signal(barrier, inc=1, device_id={"tm": target[side]}, device_id_type=MESH)
    for i in range(1, cores):
        pl.semaphore_signal(
            barrier, inc=1, device_id={"tensor": lax.rem(core + i, cores)}, device_id_type=MESH)
    neighbours = (me > 0).astype(jnp.int32) + (me < peers - 1).astype(jnp.int32)
    pl.semaphore_wait(barrier, neighbours + (cores - 1))

    def start_each(make, chunk):
        for side in range(2):
            @pl.when(has[side])
            def _():
                make(chunk, side, 1 - side).start()

    def start_bulk(chunk):
        start_each(grad_copy, chunk)
        start_each(query_copy, chunk)

    for chunk in range(min(2, chunks)):
        start_each(grad_copy, chunk)

    block = math.gcd(rows, 128)
    for index, raw in enumerate((q_raw, k_raw)):
        for top in range(0, rows, block):
            total = jnp.zeros((block, HD), jnp.float32)
            for left in range(0, width, HD):
                wide = raw[top:top + block, left:left + HD].astype(jnp.float32)
                total = total + wide * wide
            squares[core, index, top:top + block, :] = total
    for i in range(1, cores):
        square_copy(core, lax.rem(core + i, cores)).start()
    for i in range(1, cores):
        peer = lax.rem(core + i, cores)
        square_copy(core, peer).wait_send()
        square_copy(peer, peer).wait_recv()
    for index, (raw, gain, out) in enumerate(((q_raw, gain_q, q), (k_raw, gain_k, k))):
        for top in range(0, rows, block):
            total = squares[0, index, top:top + block, :]
            for other in range(1, cores):
                total = total + squares[other, index, top:top + block, :]
            mean = jnp.sum(total, axis=1, keepdims=True) / (width * cores)
            inverse = jnp.broadcast_to(lax.rsqrt(mean + EPSILON), (block, HD))
            inv[index, top:top + block, :] = inverse
            for left in range(0, width, HD):
                wide = raw[top:top + block, left:left + HD].astype(jnp.float32)
                out[top:top + block, left:left + HD] = (
                    wide * inverse * gain[:, left:left + HD]
                ).astype(out.dtype)
    for chunk in range(min(2, chunks)):
        start_each(query_copy, chunk)
    alive = tuple(
        has[side] & (
            (entries[0] == target[side]) | (entries[1] == target[side])
            | (entries[2] == target[side]))
        for side in range(2)
    )
    for side in range(2):
        @pl.when(jnp.logical_not(has[side]))
        def _():
            rq[side] = jnp.zeros(rq.shape[1:], rq.dtype)
            rg[side] = jnp.zeros(rg.shape[1:], rg.dtype)
            dq_in[side] = jnp.zeros(dq_in.shape[1:], dq_in.dtype)
            st_in[side] = jnp.zeros(st_in.shape[1:], st_in.dtype)
            co_in[side] = jnp.zeros(co_in.shape[1:], co_in.dtype)

    def column(head):
        return pl.ds(pl.multiple_of(head * HD, HD), HD)

    def put_stats(ref, index, values):
        for row, value in enumerate(values):
            ref[index + (slice(row, row + 1), slice(None))] = value

    def step(s, carry):
        @pl.when(s < chunks)
        def _():
            for side in range(2):
                @pl.when(has[side])
                def _():
                    for copy in bulk(s, side, side):
                        copy.wait_recv()
            for inner in range(group):
                head = s * group + inner
                col = column(head)
                for side in range(2):
                    put_stats(st_out, (side, head), tile_stats(
                        k[:, col], v[:, col], rq[side, :, col], rg[side, :, col]))

        @pl.when((s >= 1) & (s <= chunks))
        def _():
            for side in range(2):
                @pl.when(has[side])
                def _():
                    stat_copy(s - 1, side, side).wait_recv()
            where = pl.ds((s - 1) * group, group)
            highest = st_own[where, 0:1, :]
            for side in range(2):
                highest = jnp.where(
                    alive[side], jnp.maximum(highest, st_in[side, where, 0:1, :]), highest)
            weight = jnp.exp(st_own[where, 0:1, :] - highest)
            total = weight * st_own[where, 1:2, :]
            delta = weight * st_own[where, 2:3, :]
            for side in range(2):
                weight = jnp.exp(jnp.minimum(st_in[side, where, 0:1, :] - highest, 0.0))
                total = total + jnp.where(alive[side], weight * st_in[side, where, 1:2, :], 0.0)
                delta = delta + jnp.where(alive[side], weight * st_in[side, where, 2:3, :], 0.0)
            inverse = 1.0 / total
            delta = delta * inverse
            co_own[where, 0:1, :] = highest
            co_own[where, 1:2, :] = inverse
            co_own[where, 2:3, :] = delta
            for side in range(2):
                co_out[side, where, 0:1, :] = jnp.where(alive[side], highest, DEAD)
                co_out[side, where, 1:2, :] = inverse
                co_out[side, where, 2:3, :] = delta

        @pl.when(s < chunks)
        def _():
            for side in range(2):
                @pl.when(has[side])
                def _():
                    stat_copy(s, side, 1 - side).start()

            @pl.when(s + 2 < chunks)
            def _():
                start_bulk(s + 2)
            for inner in range(group):
                head = s * group + inner
                col = column(head)
                put_stats(st_own, (head,), tile_stats(k[:, col], v[:, col], q[:, col], g[:, col]))

        @pl.when((s >= 1) & (s <= chunks))
        def _():
            for side in range(2):
                @pl.when(has[side])
                def _():
                    comb_copy(s - 1, side, 1 - side).start()

        @pl.when(s >= 2)
        def _():
            chunk = s - 2
            for side in range(2):
                @pl.when(has[side])
                def _():
                    comb_copy(chunk, side, side).wait_recv()
            for inner in range(group):
                head = chunk * group + inner
                col = column(head)
                key = k[:, col]
                value = v[:, col]
                key_total = None
                value_total = None
                for t in range(3):
                    if t < 2:
                        query, grad, stat = rq[t, :, col], rg[t, :, col], co_in.at[t]
                    else:
                        query, grad, stat = q[:, col], g[:, col], co_own
                    scores = cols_dot(key, query) * SCALE
                    probs = jnp.exp(scores - stat[head, 0:1, :]) * stat[head, 1:2, :]
                    dprobs = cols_dot(value, grad)
                    dscore = (probs * (dprobs - stat[head, 2:3, :])).astype(jnp.bfloat16)
                    probs_b = probs.astype(jnp.bfloat16)
                    value_term = jnp.dot(probs_b, grad, preferred_element_type=jnp.float32)
                    key_term = jnp.dot(dscore, query, preferred_element_type=jnp.float32)
                    value_total = value_term if t == 0 else value_total + value_term
                    key_total = key_term if t == 0 else key_total + key_term
                    result = rows_dot(key, dscore).T * SCALE
                    if t < 2:
                        dq_out[t, :, col] = result.astype(dq_out.dtype)
                    else:
                        dq[:, col] = result
                dk[:, col] = key_total * SCALE
                dv[:, col] = value_total.astype(dv.dtype)
            for side in range(2):
                @pl.when(has[side])
                def _():
                    dq_copy(chunk, side, 1 - side).start()
        return carry

    lax.fori_loop(0, chunks + 2, step, 0)

    def drain(chunk, carry):
        for side in range(2):
            @pl.when(has[side])
            def _():
                dq_copy(chunk, side, side).wait_recv()
        where = part(chunk)
        dq[:, where] = (
            dq[:, where]
            + dq_in[0, :, where].astype(jnp.float32)
            + dq_in[1, :, where].astype(jnp.float32)
        )
        for side in range(2):
            @pl.when(has[side])
            def _():
                for copy in bulk(chunk, side, 1 - side):
                    copy.wait_send()
                stat_copy(chunk, side, 1 - side).wait_send()
                comb_copy(chunk, side, 1 - side).wait_send()
                dq_copy(chunk, side, 1 - side).wait_send()
        return carry

    lax.fori_loop(0, chunks, drain, 0)


def attention(entries, query, key, value, grad, gain_q, gain_k):
    rows, width = query.shape
    heads = width // HD
    group = math.gcd(GROUP, heads)
    chunks = heads // group
    cores = lax.axis_size("tensor")
    whole = pl.BlockSpec(memory_space=pltpu.VMEM)
    stat = (heads, STATS, rows)
    dma = pltpu.SemaphoreType.DMA

    def body(*refs):
        attention_body(group, chunks, *refs)

    return pl.pallas_call(
        body,
        out_shape=[
            jax.ShapeDtypeStruct((rows, width), jnp.float32),
            jax.ShapeDtypeStruct((rows, width), jnp.float32),
            jax.ShapeDtypeStruct((rows, width), jnp.bfloat16),
            jax.ShapeDtypeStruct((2, rows, HD), jnp.float32),
        ],
        in_specs=[pl.BlockSpec(memory_space=pltpu.SMEM)] + [whole] * 6,
        out_specs=[whole] * 4,
        scratch_shapes=[
            pltpu.VMEM((rows, width), jnp.bfloat16),
            pltpu.VMEM((rows, width), jnp.bfloat16),
            pltpu.VMEM((cores, 2, rows, HD), jnp.float32),
            dma((cores,)), dma((cores,)),
            pltpu.VMEM((2, rows, width), jnp.bfloat16),
            pltpu.VMEM((2, rows, width), jnp.bfloat16),
            pltpu.VMEM(stat, jnp.float32),
            pltpu.VMEM((2,) + stat, jnp.float32),
            pltpu.VMEM((2,) + stat, jnp.float32),
            pltpu.VMEM(stat, jnp.float32),
            pltpu.VMEM((2,) + stat, jnp.float32),
            pltpu.VMEM((2,) + stat, jnp.float32),
            pltpu.VMEM((2, rows, width), jnp.bfloat16),
            pltpu.VMEM((2, rows, width), jnp.bfloat16),
            dma((2, 2, chunks)), dma((2, 2, chunks)),
            dma((2, chunks)), dma((2, chunks)),
            dma((2, chunks)), dma((2, chunks)),
            dma((2, chunks)), dma((2, chunks)),
        ],
        compiler_params=pltpu.CompilerParams(collective_id=0, has_side_effects=True),
        name="attention",
    )(entries, query, key, value, grad, gain_q, gain_k)


def totals_body(gains, proj, gain_sum, proj_sum, gain_slots, proj_slots,
                gain_send, gain_recv, proj_send, proj_recv):
    tm = lax.axis_size("tm")
    count = lax.axis_size("batch") * tm
    me = lax.axis_index("batch") * tm + lax.axis_index("tm")
    cores = lax.axis_size("tensor")
    core = lax.axis_index("tensor")
    barrier = pltpu.get_barrier_semaphore()

    def gain_peer(i):
        return lax.rem(me + i, count)

    def gain_id(peer):
        return {"batch": lax.div(peer, tm), "tm": lax.rem(peer, tm)}

    def core_peer(i):
        return lax.rem(core + i, cores)

    def greet_gain(i, carry):
        pl.semaphore_signal(barrier, inc=1, device_id=gain_id(gain_peer(i)), device_id_type=MESH)
        return carry

    def greet_core(i, carry):
        pl.semaphore_signal(barrier, inc=1, device_id={"tensor": core_peer(i)}, device_id_type=MESH)
        return carry

    lax.fori_loop(1, count, greet_gain, 0)
    lax.fori_loop(1, cores, greet_core, 0)
    gain_slots[me] = gains[...]
    proj_slots[core] = proj[...]
    pl.semaphore_wait(barrier, count - 1 + cores - 1)

    def gain_copy(slot, peer):
        return pltpu.make_async_remote_copy(
            src_ref=gains, dst_ref=gain_slots.at[slot], send_sem=gain_send.at[peer],
            recv_sem=gain_recv.at[slot], device_id=gain_id(peer), device_id_type=MESH,
        )

    def proj_copy(slot, peer):
        return pltpu.make_async_remote_copy(
            src_ref=proj, dst_ref=proj_slots.at[slot], send_sem=proj_send.at[peer],
            recv_sem=proj_recv.at[slot], device_id={"tensor": peer}, device_id_type=MESH,
        )

    def send_core(i, carry):
        proj_copy(core, core_peer(i)).start()
        return carry

    def send_gain(i, carry):
        gain_copy(me, gain_peer(i)).start()
        return carry

    def end_core(i, carry):
        peer = core_peer(i)
        proj_copy(core, peer).wait_send()
        proj_copy(peer, peer).wait_recv()
        return carry

    def end_gain(i, carry):
        peer = gain_peer(i)
        gain_copy(me, peer).wait_send()
        gain_copy(peer, peer).wait_recv()
        return carry

    lax.fori_loop(1, cores, send_core, 0)
    lax.fori_loop(1, count, send_gain, 0)
    lax.fori_loop(1, cores, end_core, 0)
    lax.fori_loop(1, count, end_gain, 0)
    proj_sum[...] = jnp.sum(proj_slots[...], axis=0)
    gain_sum[...] = jnp.sum(gain_slots[...], axis=0)


def totals(gains, proj):
    count = lax.axis_size("batch") * lax.axis_size("tm")
    cores = lax.axis_size("tensor")
    whole = pl.BlockSpec(memory_space=pltpu.VMEM)
    dma = pltpu.SemaphoreType.DMA
    return pl.pallas_call(
        totals_body,
        out_shape=[
            jax.ShapeDtypeStruct(gains.shape, jnp.float32),
            jax.ShapeDtypeStruct(proj.shape, jnp.float32),
        ],
        in_specs=[whole] * 2,
        out_specs=[whole] * 2,
        scratch_shapes=[
            pltpu.VMEM((count,) + gains.shape, jnp.float32),
            pltpu.VMEM((cores,) + proj.shape, jnp.float32),
            dma((count,)), dma((count,)), dma((cores,)), dma((cores,)),
        ],
        compiler_params=pltpu.CompilerParams(collective_id=1, has_side_effects=True),
        name="totals",
    )(gains, proj)


def finish_norm(wide_rows, inverse, gain_row, grad_normed, projection, feature_count):
    cubed = inverse * inverse * inverse
    grad_rows = (
        inverse[:, None] * gain_row[None, :] * grad_normed
        - wide_rows * (cubed * projection / feature_count)[:, None]
    )
    return grad_rows.astype(jnp.bfloat16)


def shards(q_raw, k_raw, values, grad_out, gain_q, gain_k, tile_lists):
    query_wide = q_raw[0].astype(jnp.float32)
    key_wide = k_raw[0].astype(jnp.float32)
    value_rows = values[0]
    grad_rows = grad_out[0]
    entries = tile_lists[0, 0]
    token_count, feature_count = query_wide.shape
    width_all = feature_count * lax.axis_size("tensor")
    count_all = lax.axis_size("batch") * lax.axis_size("tm") * token_count
    grad_query, grad_kn, grad_values, inverse = attention(
        entries, q_raw[0], k_raw[0], value_rows, grad_rows, gain_q[None], gain_k[None]
    )
    inverse_q = inverse[0, :, 0]
    inverse_k = inverse[1, :, 0]
    gain_terms, proj = totals(
        jnp.stack(
            [
                jnp.sum(grad_query * query_wide * inverse_q[:, None], axis=0),
                jnp.sum(grad_kn * key_wide * inverse_k[:, None], axis=0),
            ]
        ),
        jnp.stack(
            [
                jnp.sum(query_wide * gain_q[None, :] * grad_query, axis=1),
                jnp.sum(key_wide * gain_k[None, :] * grad_kn, axis=1),
            ]
        ),
    )
    grad_q = finish_norm(query_wide, inverse_q, gain_q, grad_query, proj[0], width_all)
    grad_k = finish_norm(key_wide, inverse_k, gain_k, grad_kn, proj[1], width_all)
    factor_all = 1.0 / math.sqrt(count_all)
    return (
        grad_q[None],
        grad_k[None],
        grad_values[None],
        gain_terms[0] * factor_all,
        gain_terms[1] * factor_all,
    )


def solution(mesh):
    rows = P("batch", "tm", "tensor")
    return jax.shard_map(
        shards,
        mesh=mesh,
        in_specs=(rows, rows, rows, rows, P("tensor"), P("tensor"), P("batch", "tm", None)),
        out_specs=(rows, rows, rows, P("tensor"), P("tensor")),
        check_vma=False,
    )
```

```python
import math

import jax
import jax.numpy as jnp
from jax import lax
from jax.experimental import pallas as pl
from jax.experimental.pallas import tpu as pltpu
from jax.sharding import PartitionSpec as P

HD = 128
STATS = 4
EPSILON = 1e-06
DEAD = 1e30
SCALE = HD ** (-0.5)
GROUP = 2
MESH = pl.DeviceIdType.MESH


def cols_dot(left, right):
    return lax.dot_general(
        left, right, (((1,), (1,)), ((), ())), preferred_element_type=jnp.float32
    )


def rows_dot(left, right):
    return lax.dot_general(
        left, right, (((0,), (0,)), ((), ())), preferred_element_type=jnp.float32
    )


def tile_stats(key, value, query, grad):
    scores = cols_dot(key, query) * SCALE
    highest = jnp.max(scores, axis=0, keepdims=True)
    exponent = jnp.exp(scores - highest)
    dprobs = cols_dot(value, grad)
    total = jnp.sum(exponent, axis=0, keepdims=True)
    weighted = jnp.sum(exponent * dprobs, axis=0, keepdims=True)
    return highest, total, weighted


def attention_body(group, chunks, entries, q_raw, k_raw, v, g, gain_q, gain_k,
                   grad_q, grad_k, dv, gain_sum,
                   dq, dk, inv, proj, terms, pj_send, pj_recv, tm_send, tm_recv,
                   q, k, squares, sq_send, sq_recv, rq, rg, st_own, st_out, st_in, co_own, co_out, co_in, dq_out, dq_in,
                   bulk_send, bulk_recv, st_send, st_recv, co_send, co_recv, dq_send, dq_recv):
    rows, width = q.shape
    span = group * HD
    core = lax.axis_index("tensor")
    cores = lax.axis_size("tensor")
    me = lax.axis_index("tm")
    peers = lax.axis_size("tm")
    has = (me > 0, me < peers - 1)
    target = (jnp.maximum(me - 1, 0), jnp.minimum(me + 1, peers - 1))

    def part(chunk):
        return pl.ds(pl.multiple_of(chunk * span, HD), span)

    def remote(source, sink, send, recv, side):
        return pltpu.make_async_remote_copy(
            src_ref=source, dst_ref=sink, send_sem=send, recv_sem=recv,
            device_id={"tm": target[side]}, device_id_type=MESH,
        )

    def grad_copy(chunk, side, slot):
        where = part(chunk)
        return remote(g.at[:, where], rg.at[slot, :, where],
                      bulk_send.at[side, 0, chunk], bulk_recv.at[slot, 0, chunk], side)

    def query_copy(chunk, side, slot):
        where = part(chunk)
        return remote(q.at[:, where], rq.at[slot, :, where],
                      bulk_send.at[side, 1, chunk], bulk_recv.at[slot, 1, chunk], side)

    def bulk(chunk, side, slot):
        return grad_copy(chunk, side, slot), query_copy(chunk, side, slot)

    def square_copy(slot, peer):
        return pltpu.make_async_remote_copy(
            src_ref=squares.at[slot], dst_ref=squares.at[slot], send_sem=sq_send.at[peer],
            recv_sem=sq_recv.at[slot], device_id={"tensor": peer}, device_id_type=MESH,
        )

    def small(out, into, send, recv, chunk, side, slot):
        where = pl.ds(chunk * group, group)
        return remote(out.at[side, where], into.at[slot, where],
                      send.at[side, chunk], recv.at[slot, chunk], side)

    def stat_copy(chunk, side, slot):
        return small(st_out, st_in, st_send, st_recv, chunk, side, slot)

    def comb_copy(chunk, side, slot):
        return small(co_out, co_in, co_send, co_recv, chunk, side, slot)

    def dq_copy(chunk, side, slot):
        where = part(chunk)
        return remote(dq_out.at[side, :, where], dq_in.at[slot, :, where],
                      dq_send.at[side, chunk], dq_recv.at[slot, chunk], side)

    count = lax.axis_size("batch") * peers
    rank = lax.axis_index("batch") * peers + me

    def other_rank(i):
        return lax.rem(rank + i, count)

    def rank_id(peer):
        return {"batch": lax.div(peer, peers), "tm": lax.rem(peer, peers)}

    def proj_copy(slot, peer):
        return pltpu.make_async_remote_copy(
            src_ref=proj.at[slot], dst_ref=proj.at[slot], send_sem=pj_send.at[peer],
            recv_sem=pj_recv.at[slot], device_id={"tensor": peer}, device_id_type=MESH,
        )

    def term_copy(slot, peer):
        return pltpu.make_async_remote_copy(
            src_ref=terms.at[slot], dst_ref=terms.at[slot], send_sem=tm_send.at[peer],
            recv_sem=tm_recv.at[slot], device_id=rank_id(peer), device_id_type=MESH,
        )

    barrier = pltpu.get_barrier_semaphore()

    def greet(i, carry):
        pl.semaphore_signal(
            barrier, inc=1, device_id=rank_id(other_rank(i)), device_id_type=MESH)
        return carry

    lax.fori_loop(1, count, greet, 0)
    for i in range(1, cores):
        pl.semaphore_signal(
            barrier, inc=1, device_id={"tensor": lax.rem(core + i, cores)}, device_id_type=MESH)
    pl.semaphore_wait(barrier, count - 1 + cores - 1)

    def start_each(make, chunk):
        for side in range(2):
            @pl.when(has[side])
            def _():
                make(chunk, side, 1 - side).start()

    def start_bulk(chunk):
        start_each(grad_copy, chunk)
        start_each(query_copy, chunk)

    for chunk in range(min(2, chunks)):
        start_each(grad_copy, chunk)

    block = math.gcd(rows, 128)
    for index, raw in enumerate((q_raw, k_raw)):
        for top in range(0, rows, block):
            total = jnp.zeros((block, HD), jnp.float32)
            for left in range(0, width, HD):
                wide = raw[top:top + block, left:left + HD].astype(jnp.float32)
                total = total + wide * wide
            squares[core, index, top:top + block, :] = total
    for i in range(1, cores):
        square_copy(core, lax.rem(core + i, cores)).start()
    for i in range(1, cores):
        peer = lax.rem(core + i, cores)
        square_copy(core, peer).wait_send()
        square_copy(peer, peer).wait_recv()
    for index, (raw, gain, out) in enumerate(((q_raw, gain_q, q), (k_raw, gain_k, k))):
        for top in range(0, rows, block):
            total = squares[0, index, top:top + block, :]
            for other in range(1, cores):
                total = total + squares[other, index, top:top + block, :]
            mean = jnp.sum(total, axis=1, keepdims=True) / (width * cores)
            inverse = jnp.broadcast_to(lax.rsqrt(mean + EPSILON), (block, HD))
            inv[index, top:top + block, :] = inverse
            for left in range(0, width, HD):
                wide = raw[top:top + block, left:left + HD].astype(jnp.float32)
                out[top:top + block, left:left + HD] = (
                    wide * inverse * gain[left // HD:left // HD + 1, :]
                ).astype(out.dtype)
    for chunk in range(min(2, chunks)):
        start_each(query_copy, chunk)
    alive = tuple(
        has[side] & (
            (entries[0] == target[side]) | (entries[1] == target[side])
            | (entries[2] == target[side]))
        for side in range(2)
    )
    for side in range(2):
        @pl.when(jnp.logical_not(has[side]))
        def _():
            rq[side] = jnp.zeros(rq.shape[1:], rq.dtype)
            rg[side] = jnp.zeros(rg.shape[1:], rg.dtype)
            dq_in[side] = jnp.zeros(dq_in.shape[1:], dq_in.dtype)
            st_in[side] = jnp.zeros(st_in.shape[1:], st_in.dtype)
            co_in[side] = jnp.zeros(co_in.shape[1:], co_in.dtype)

    def column(head):
        return pl.ds(pl.multiple_of(head * HD, HD), HD)

    def put_stats(ref, index, values):
        for row, value in enumerate(values):
            ref[index + (slice(row, row + 1), slice(None))] = value

    def step(s, carry):
        @pl.when(s < chunks)
        def _():
            for side in range(2):
                @pl.when(has[side])
                def _():
                    for copy in bulk(s, side, side):
                        copy.wait_recv()
            for inner in range(group):
                head = s * group + inner
                col = column(head)
                for side in range(2):
                    put_stats(st_out, (side, head), tile_stats(
                        k[:, col], v[:, col], rq[side, :, col], rg[side, :, col]))

        @pl.when((s >= 1) & (s <= chunks))
        def _():
            for side in range(2):
                @pl.when(has[side])
                def _():
                    stat_copy(s - 1, side, side).wait_recv()
            where = pl.ds((s - 1) * group, group)
            highest = st_own[where, 0:1, :]
            for side in range(2):
                highest = jnp.where(
                    alive[side], jnp.maximum(highest, st_in[side, where, 0:1, :]), highest)
            weight = jnp.exp(st_own[where, 0:1, :] - highest)
            total = weight * st_own[where, 1:2, :]
            delta = weight * st_own[where, 2:3, :]
            for side in range(2):
                weight = jnp.exp(jnp.minimum(st_in[side, where, 0:1, :] - highest, 0.0))
                total = total + jnp.where(alive[side], weight * st_in[side, where, 1:2, :], 0.0)
                delta = delta + jnp.where(alive[side], weight * st_in[side, where, 2:3, :], 0.0)
            inverse = 1.0 / total
            delta = delta * inverse
            co_own[where, 0:1, :] = highest
            co_own[where, 1:2, :] = inverse
            co_own[where, 2:3, :] = delta
            for side in range(2):
                co_out[side, where, 0:1, :] = jnp.where(alive[side], highest, DEAD)
                co_out[side, where, 1:2, :] = inverse
                co_out[side, where, 2:3, :] = delta

        @pl.when(s < chunks)
        def _():
            for side in range(2):
                @pl.when(has[side])
                def _():
                    stat_copy(s, side, 1 - side).start()

            @pl.when(s + 2 < chunks)
            def _():
                start_bulk(s + 2)
            for inner in range(group):
                head = s * group + inner
                col = column(head)
                put_stats(st_own, (head,), tile_stats(k[:, col], v[:, col], q[:, col], g[:, col]))

        @pl.when((s >= 1) & (s <= chunks))
        def _():
            for side in range(2):
                @pl.when(has[side])
                def _():
                    comb_copy(s - 1, side, 1 - side).start()

        @pl.when(s >= 2)
        def _():
            chunk = s - 2
            for side in range(2):
                @pl.when(has[side])
                def _():
                    comb_copy(chunk, side, side).wait_recv()
            for inner in range(group):
                head = chunk * group + inner
                col = column(head)
                key = k[:, col]
                value = v[:, col]
                key_total = None
                value_total = None
                for t in range(3):
                    if t < 2:
                        query, grad, stat = rq[t, :, col], rg[t, :, col], co_in.at[t]
                    else:
                        query, grad, stat = q[:, col], g[:, col], co_own
                    scores = cols_dot(key, query) * SCALE
                    probs = jnp.exp(scores - stat[head, 0:1, :]) * stat[head, 1:2, :]
                    dprobs = cols_dot(value, grad)
                    dscore = (probs * (dprobs - stat[head, 2:3, :])).astype(jnp.bfloat16)
                    probs_b = probs.astype(jnp.bfloat16)
                    value_term = jnp.dot(probs_b, grad, preferred_element_type=jnp.float32)
                    key_term = jnp.dot(dscore, query, preferred_element_type=jnp.float32)
                    value_total = value_term if t == 0 else value_total + value_term
                    key_total = key_term if t == 0 else key_total + key_term
                    result = rows_dot(key, dscore).T * SCALE
                    if t < 2:
                        dq_out[t, :, col] = result.astype(dq_out.dtype)
                    else:
                        dq[:, col] = result
                dk[:, col] = key_total * SCALE
                dv[:, col] = value_total.astype(dv.dtype)
            for side in range(2):
                @pl.when(has[side])
                def _():
                    dq_copy(chunk, side, 1 - side).start()
        return carry

    lax.fori_loop(0, chunks + 2, step, 0)

    def drain(chunk, carry):
        for side in range(2):
            @pl.when(has[side])
            def _():
                dq_copy(chunk, side, side).wait_recv()
        where = part(chunk)
        dq[:, where] = (
            dq[:, where]
            + dq_in[0, :, where].astype(jnp.float32)
            + dq_in[1, :, where].astype(jnp.float32)
        )
        for side in range(2):
            @pl.when(has[side])
            def _():
                for copy in bulk(chunk, side, 1 - side):
                    copy.wait_send()
                stat_copy(chunk, side, 1 - side).wait_send()
                comb_copy(chunk, side, 1 - side).wait_send()
                dq_copy(chunk, side, 1 - side).wait_send()
        return carry

    lax.fori_loop(0, chunks, drain, 0)
    heads = width // HD
    sides = ((q_raw, gain_q, dq, grad_q), (k_raw, gain_k, dk, grad_k))
    for index, (raw, gain, normed, out) in enumerate(sides):
        proj[core, index] = jnp.zeros((rows, HD), jnp.float32)

        def reduce(head, carry):
            col = column(head)
            both = raw[:, col].astype(jnp.float32) * normed[:, col]
            terms[rank, index, pl.ds(head, 1), :] = jnp.sum(
                both * inv[index], axis=0, keepdims=True)
            proj[core, index] = proj[core, index] + both * gain[pl.ds(head, 1), :]
            return carry

        lax.fori_loop(0, heads, reduce, 0)
    for i in range(1, cores):
        proj_copy(core, lax.rem(core + i, cores)).start()

    def send_terms(i, carry):
        term_copy(rank, other_rank(i)).start()
        return carry

    lax.fori_loop(1, count, send_terms, 0)
    for i in range(1, cores):
        peer = lax.rem(core + i, cores)
        proj_copy(core, peer).wait_send()
        proj_copy(peer, peer).wait_recv()
    for index, (raw, gain, normed, out) in enumerate(sides):
        for top in range(0, rows, block):
            total = proj[0, index, top:top + block, :]
            for other in range(1, cores):
                total = total + proj[other, index, top:top + block, :]
            inverse = inv[index, top:top + block, :]
            projection = jnp.sum(total, axis=1, keepdims=True)
            pull = inverse * inverse * inverse * projection / (width * cores)
            for left in range(0, width, HD):
                wide = raw[top:top + block, left:left + HD].astype(jnp.float32)
                out[top:top + block, left:left + HD] = (
                    inverse * gain[left // HD:left // HD + 1, :]
                    * normed[top:top + block, left:left + HD] - wide * pull
                ).astype(out.dtype)

    def end_terms(i, carry):
        peer = other_rank(i)
        term_copy(rank, peer).wait_send()
        term_copy(peer, peer).wait_recv()
        return carry

    lax.fori_loop(1, count, end_terms, 0)
    gain_sum[...] = jnp.sum(terms[...], axis=0) * (1.0 / math.sqrt(count * rows))


def attention(entries, query, key, value, grad, gain_q, gain_k):
    rows, width = query.shape
    heads = width // HD
    group = math.gcd(GROUP, heads)
    chunks = heads // group
    cores = lax.axis_size("tensor")
    count = lax.axis_size("batch") * lax.axis_size("tm")
    whole = pl.BlockSpec(memory_space=pltpu.VMEM)
    stat = (heads, STATS, rows)
    dma = pltpu.SemaphoreType.DMA

    def body(*refs):
        attention_body(group, chunks, *refs)

    return pl.pallas_call(
        body,
        out_shape=[
            jax.ShapeDtypeStruct((rows, width), jnp.bfloat16),
            jax.ShapeDtypeStruct((rows, width), jnp.bfloat16),
            jax.ShapeDtypeStruct((rows, width), jnp.bfloat16),
            jax.ShapeDtypeStruct((2, heads, HD), jnp.float32),
        ],
        in_specs=[pl.BlockSpec(memory_space=pltpu.SMEM)] + [whole] * 6,
        out_specs=[whole] * 4,
        scratch_shapes=[
            pltpu.VMEM((rows, width), jnp.float32),
            pltpu.VMEM((rows, width), jnp.float32),
            pltpu.VMEM((2, rows, HD), jnp.float32),
            pltpu.VMEM((cores, 2, rows, HD), jnp.float32),
            pltpu.VMEM((count, 2, heads, HD), jnp.float32),
            dma((cores,)), dma((cores,)), dma((count,)), dma((count,)),
            pltpu.VMEM((rows, width), jnp.bfloat16),
            pltpu.VMEM((rows, width), jnp.bfloat16),
            pltpu.VMEM((cores, 2, rows, HD), jnp.float32),
            dma((cores,)), dma((cores,)),
            pltpu.VMEM((2, rows, width), jnp.bfloat16),
            pltpu.VMEM((2, rows, width), jnp.bfloat16),
            pltpu.VMEM(stat, jnp.float32),
            pltpu.VMEM((2,) + stat, jnp.float32),
            pltpu.VMEM((2,) + stat, jnp.float32),
            pltpu.VMEM(stat, jnp.float32),
            pltpu.VMEM((2,) + stat, jnp.float32),
            pltpu.VMEM((2,) + stat, jnp.float32),
            pltpu.VMEM((2, rows, width), jnp.bfloat16),
            pltpu.VMEM((2, rows, width), jnp.bfloat16),
            dma((2, 2, chunks)), dma((2, 2, chunks)),
            dma((2, chunks)), dma((2, chunks)),
            dma((2, chunks)), dma((2, chunks)),
            dma((2, chunks)), dma((2, chunks)),
        ],
        compiler_params=pltpu.CompilerParams(collective_id=0, has_side_effects=True),
        name="attention",
    )(entries, query, key, value, grad, gain_q, gain_k)


def shards(q_raw, k_raw, values, grad_out, gain_q, gain_k, tile_lists):
    width = q_raw.shape[2]
    heads = width // HD
    grad_q, grad_k, grad_values, gain_sum = attention(
        tile_lists[0, 0], q_raw[0], k_raw[0], values[0], grad_out[0],
        gain_q.reshape(heads, HD), gain_k.reshape(heads, HD),
    )
    return (
        grad_q[None],
        grad_k[None],
        grad_values[None],
        gain_sum[0].reshape(width),
        gain_sum[1].reshape(width),
    )


def solution(mesh):
    rows = P("batch", "tm", "tensor")
    return jax.shard_map(
        shards,
        mesh=mesh,
        in_specs=(rows, rows, rows, rows, P("tensor"), P("tensor"), P("batch", "tm", None)),
        out_specs=(rows, rows, rows, P("tensor"), P("tensor")),
        check_vma=False,
    )
```
